32 devices in a mesh: patch: 2 (over y), visit: 4 (over z), tile: 4 (over x, core).
Axes of the slice: x: 2, y: 2, z: 4, core: 2. Of those that a mesh axis runs over, the one named last changes fastest.
Arguments:
- exposure: float32 [16, 256, 4096], P('visit', ('patch', 'tile')), parts along dimension 1, may hold values from -12 to 12
- variance: float32 [16, 256, 4096], P('visit', ('patch', 'tile')), parts along dimension 1, may hold values from 0.25 to 4
- usable: int32 [16, 256, 4096], P('visit', ('patch', 'tile')), parts along dimension 1, may hold values from 0 to 1, as said below
- basis_width: float32 [32, 3], P(('patch', 'visit')), parts along dimension 0, may hold values from 0.8 to 3.5
- spatial_coef: float32 [32, 3, 6], P(('patch', 'visit')), parts along dimension 0, may hold values from -0.6 to 1.4
Outputs:
- coadd: float32 [256, 4096], P(('patch', 'tile')), parts along dimension 0
The draws below stay inside these ranges and needn't reach their ends.
There are 2 independent parts, one for each index of `patch`. The reference program is written for one: setup_inputs(seed, part) draws one part's arguments, and reference() takes and returns one part's arrays. A program takes and returns all parts, laid end to end along the dimension named above; each array names one. Nothing has to cross between parts.
Inputs may be any that keep to these rules, and one draw needn't show every extreme that they name: 1 marks a usable sample; at every pixel at least 5 of the 16 visits are usable.
All inputs are finite; a program needn't handle non-finite values.
Results may differ from the reference program's by a relative error of at most 0.0003.
Values sent between devices are 32-bit elements; how exact they have to be, the bound alone decides.
No kernel may reach another device: no remote copies, remote signals or barrier semaphores. Data moves between devices by JAX's collectives and lax.ppermute only.
A program may use at most 128 MiB of HBM per device.

```python
import math
import jax
import jax.numpy as jnp
from jax import lax

W = 4096
KHALF = 15
BASES = 3
TERMS = 6
VISITS = 16
ROWS = 128


def draw_exposure(key, part):
    base_key = jax.random.fold_in(key, 11)
    sky_key, noise_key, hit_key = jax.random.split(base_key, 3)
    sky_field = jax.random.normal(sky_key, (ROWS, W), jnp.float32)
    hits = (jax.random.randint(hit_key, (VISITS, ROWS, W), 0, 64) == 0).astype(jnp.float32)
    noise = jax.random.normal(noise_key, (VISITS, ROWS, W), jnp.float32)
    sky_field = 1.5 * sky_field
    return jnp.clip(sky_field[None] + noise + 6.0 * hits, -12.0, 12.0)


def draw_usable(key, part):
    base_key = jax.random.fold_in(key, 23)
    rough_key, offset_key = jax.random.split(base_key, 2)
    rough = jax.random.randint(rough_key, (VISITS, ROWS, W), 0, 8) != 0
    offset = jax.random.randint(offset_key, (ROWS, W), 0, VISITS)
    visit_ids = jnp.arange(VISITS).astype(jnp.int32)[:, None, None]
    kept = (visit_ids - offset[None]) % VISITS < 5
    return jnp.logical_or(rough, kept).astype(jnp.int32)


def draw_spatial_coef(key, part):
    base_key = jax.random.fold_in(key, 37)
    rest_key, main_key = jax.random.split(base_key, 2)
    rest = jnp.clip(0.15 * jax.random.normal(rest_key, (VISITS, BASES, TERMS), jnp.float32), -0.6, 0.6)
    main = jnp.clip(1.0 + 0.1 * jax.random.normal(main_key, (VISITS,), jnp.float32), 0.6, 1.4)
    return rest.at[:, 0, 0].set(main)


def block_scale(key, dims, pieces, low, high):
    factor_of, own = 1.0, jax.random.fold_in(key, 6)
    for position, blocks in pieces:
        steps = jnp.exp(jax.random.uniform(jax.random.fold_in(own, position), (blocks,), jnp.float32, low / len(pieces), high / len(pieces)))
        factor_of = factor_of * jnp.repeat(steps, dims[position] // blocks).reshape([-1 if axis == position else 1 for axis in range(len(dims))])
    return factor_of


def setup_inputs(seed: int = 0, part: int = 0) -> dict:
    splits = jax.random.split(jax.random.key(seed), 6)
    part_splits = jax.random.split(jax.random.fold_in(splits[5], part), 6)
    exposure = draw_exposure(jax.random.fold_in(jax.random.fold_in(splits[5], part), 71), part)
    variance = jnp.clip(jnp.exp(math.log(4.0) - 2.7725887 * jax.random.uniform(part_splits[1], (VISITS, ROWS, W), jnp.float32) ** block_scale(part_splits[1], (VISITS, ROWS, W), ((0, 4), (1, 4)), -0.2, 0.2)), 0.25, 4.0)
    usable = draw_usable(jax.random.fold_in(jax.random.fold_in(splits[5], part), 71), part)
    basis_width = jnp.clip(jnp.exp(math.log(3.5) - 1.4759065 * jax.random.uniform(part_splits[3], (VISITS, BASES), jnp.float32) ** block_scale(part_splits[3], (VISITS, BASES), ((0, 4),), -0.2, 0.2)), 0.8, 3.5)
    spatial_coef = draw_spatial_coef(jax.random.fold_in(jax.random.fold_in(splits[5], part), 71), part)
    return {"exposure": exposure, "variance": variance, "usable": usable, "basis_width": basis_width, "spatial_coef": spatial_coef}


def basis_profile(offsets, width, basis_id):
    profile = jnp.exp(-offsets * offsets / (2.0 * width * width))
    if basis_id > 0:
        profile = profile * (offsets / width) ** (2 * basis_id)
    return profile


def reference(exposure, variance, usable, basis_width, spatial_coef):
    offsets = jnp.arange(-KHALF, KHALF + 1).astype(jnp.float32)
    row_pos = 2.0 * jnp.arange(ROWS).astype(jnp.float32) / (ROWS - 1) - 1.0
    col_pos = 2.0 * jnp.arange(W).astype(jnp.float32) / (W - 1) - 1.0
    ycoord = jnp.broadcast_to(row_pos[:, None], (ROWS, W))
    xcoord = jnp.broadcast_to(col_pos[None, :], (ROWS, W))
    poly_terms = [jnp.ones((ROWS, W), jnp.float32), xcoord, ycoord, xcoord * xcoord, xcoord * ycoord, ycoord * ycoord]

    def one_visit(inputs):
        image, widths, coefs = inputs
        padded = jnp.pad(image, KHALF)
        matched = jnp.zeros((ROWS, W), jnp.float32)
        for basis_id in range(BASES):
            profile = basis_profile(offsets, widths[basis_id], basis_id)
            profile = profile / jnp.sum(profile)
            vertical = jnp.zeros((ROWS, W + 2 * KHALF), jnp.float32)
            for shift_id in range(2 * KHALF + 1):
                vertical = vertical + profile[shift_id] * padded[shift_id:shift_id + ROWS, :]
            smoothed = jnp.zeros((ROWS, W), jnp.float32)
            for shift_id in range(2 * KHALF + 1):
                smoothed = smoothed + profile[shift_id] * vertical[:, shift_id:shift_id + W]
            factor = jnp.zeros((ROWS, W), jnp.float32)
            for term_id in range(TERMS):
                factor = factor + coefs[basis_id, term_id] * poly_terms[term_id]
            matched = matched + factor * smoothed
        return matched

    matched = lax.map(one_visit, (exposure, basis_width, spatial_coef))
    valid = usable > 0
    big_value = 1e30
    lower = jnp.sort(jnp.where(valid, matched, big_value), axis=0)[2]
    upper = jnp.sort(jnp.where(valid, matched, -big_value), axis=0)[-3]
    weight = jnp.where(valid, 1.0 / variance, 0.0)
    numer = jnp.sum(weight * jnp.clip(matched, lower, upper), axis=0)
    denom = jnp.sum(weight, axis=0)
    return numer / denom
```

```python
import functools
import jax
import jax.numpy as jnp
from jax import lax
from jax.experimental import pallas as pl
from jax.experimental.pallas import tpu as pltpu
from jax.sharding import PartitionSpec as P

KHALF = 15
BASES = 3
HALO = 16
LANES = 128
big_value = 1e30


def profile_of(offsets, width, basis_id):
    ratio = (offsets / width) * (offsets / width)
    profile = jnp.exp(-0.5 * ratio)
    for _ in range(basis_id):
        profile = profile * ratio
    return jnp.where(jnp.abs(offsets) <= KHALF, profile, 0.0)


def split(values):
    high = values.astype(jnp.bfloat16)
    low = (values - high.astype(jnp.float32)).astype(jnp.bfloat16)
    return high, low


def prep_kernel(rows, width_ref, down_ref, across_ref):
    visit = pl.program_id(0)
    depth = rows + 2 * HALO
    tap = lax.broadcasted_iota(jnp.int32, (8, LANES), 1) - KHALF
    first = lax.broadcasted_iota(jnp.int32, (8, LANES), 0) == 0
    for basis_id in range(BASES):
        width = jnp.full((1, 1), width_ref[visit, basis_id], jnp.float32)
        raw = profile_of(tap.astype(jnp.float32), width, basis_id)
        total = jnp.sum(jnp.where(first, raw, 0.0), axis=(0, 1), keepdims=True)
        inverse = 1.0 / total
        in_row = lax.broadcasted_iota(jnp.int32, (rows, depth), 1)
        out_row = lax.broadcasted_iota(jnp.int32, (rows, depth), 0)
        offsets = (in_row - out_row - HALO).astype(jnp.float32)
        high, low = split(profile_of(offsets, width, basis_id) * inverse)
        here = pl.ds(basis_id * rows, rows)
        down_ref[0, here, :] = jnp.concatenate([high, low, high], axis=1)
        in_col = lax.broadcasted_iota(jnp.int32, (3 * LANES, LANES), 0)
        out_col = lax.broadcasted_iota(jnp.int32, (3 * LANES, LANES), 1)
        offsets = (in_col - out_col - LANES).astype(jnp.float32)
        high, low = split(profile_of(offsets, width, basis_id) * inverse)
        across_ref[0, basis_id, :, 0:LANES] = high
        across_ref[0, basis_id, :, LANES : 2 * LANES] = low


def prep(basis_width, rows):
    visits = basis_width.shape[0]
    depth = rows + 2 * HALO
    return pl.pallas_call(
        functools.partial(prep_kernel, rows),
        grid=(visits,),
        in_specs=[pl.BlockSpec(memory_space=pltpu.SMEM)],
        out_specs=[
            pl.BlockSpec((1, BASES * rows, 3 * depth), lambda v: (v, 0, 0)),
            pl.BlockSpec((1, BASES, 3 * LANES, 2 * LANES), lambda v: (v, 0, 0, 0)),
        ],
        out_shape=[
            jax.ShapeDtypeStruct((visits, BASES * rows, 3 * depth), jnp.bfloat16),
            jax.ShapeDtypeStruct((visits, BASES, 3 * LANES, 2 * LANES), jnp.bfloat16),
        ],
        name="band_matrices",
    )(basis_width)


def match_kernel(
    total_rows, total_cols, where_ref,
    mid, mid_l, mid_r, up, up_l, up_r, dn, dn_l, dn_r,
    variance, usable, down, across, coef, out, stacked,
):
    visit = pl.program_id(0)
    block_id = where_ref[0]
    tile_id = where_ref[1]
    rows, cols = mid.shape[1], mid.shape[2]
    depth = rows + 2 * HALO
    pieces = cols // LANES
    left_on = jnp.where(block_id > 0, 1.0, 0.0)
    right_on = jnp.where((block_id + 1) * cols < total_cols, 1.0, 0.0)
    for part, left, right, start, count in (
        (up, up_l, up_r, 0, HALO),
        (mid, mid_l, mid_r, HALO, rows),
        (dn, dn_l, dn_r, HALO + rows, HALO),
    ):
        for source, col, wide, scale in (
            (left, 0, LANES, left_on),
            (part, LANES, cols, None),
            (right, LANES + cols, LANES, right_on),
        ):
            values = source[0]
            if scale is not None:
                values = values * scale
            high, low = split(values)
            stacked[start : start + count, col : col + wide] = high
            stacked[depth + start : depth + start + count, col : col + wide] = high
            stacked[2 * depth + start : 2 * depth + start + count, col : col + wide] = low
    vertical = jnp.dot(down[0], stacked[...], preferred_element_type=jnp.float32)
    high, low = split(vertical)
    row_id = tile_id * rows + lax.broadcasted_iota(jnp.int32, (rows, LANES), 0)
    y = 2.0 * row_id.astype(jnp.float32) / (total_rows - 1) - 1.0
    matched = [None] * pieces
    for basis_id in range(BASES):
        here = slice(basis_id * rows, (basis_id + 1) * rows)
        windows = [
            part[here, LANES * n : LANES * (n + 3)] for part in (high, low) for n in range(pieces)
        ]
        smooth = jnp.dot(
            jnp.concatenate(windows, axis=0), across[0, basis_id], preferred_element_type=jnp.float32
        )
        c = [coef[visit, basis_id, k] for k in range(6)]
        flat = c[0] + y * (c[2] + y * c[5])
        slope = c[1] + y * c[4]
        for n in range(pieces):
            top = smooth[rows * n : rows * (n + 1)]
            low_part = smooth[rows * (pieces + n) : rows * (pieces + n + 1), 0:LANES]
            value = top[:, 0:LANES] + (top[:, LANES:] + low_part)
            col_id = block_id * cols + LANES * n + lax.broadcasted_iota(jnp.int32, (rows, LANES), 1)
            x = 2.0 * col_id.astype(jnp.float32) / (total_cols - 1) - 1.0
            term = (flat + x * (slope + x * c[3])) * value
            matched[n] = term if basis_id == 0 else matched[n] + term
    for n in range(pieces):
        out[0, 0, :, LANES * n : LANES * (n + 1)] = matched[n]
    out[1, 0] = jnp.where(usable[0] > 0, 1.0 / variance[0], 0.0)


def match(where, cols, total_rows, exposure, above, below, variance, usable, down, across, coef):
    visits, rows, total_cols = exposure.shape
    per_block = cols // LANES
    last = total_cols // LANES - 1

    def main(count):
        return pl.BlockSpec((1, count, cols), lambda v, w: (v, 0, w[0]))

    def left(count):
        return pl.BlockSpec(
            (1, count, LANES), lambda v, w: (v, 0, jnp.maximum(w[0] * per_block - 1, 0))
        )

    def right(count):
        return pl.BlockSpec(
            (1, count, LANES), lambda v, w: (v, 0, jnp.minimum((w[0] + 1) * per_block, last))
        )

    def around(count):
        return [main(count), left(count), right(count)]

    depth = rows + 2 * HALO
    return pl.pallas_call(
        functools.partial(match_kernel, total_rows, total_cols),
        grid_spec=pltpu.PrefetchScalarGridSpec(
            num_scalar_prefetch=1,
            grid=(visits,),
            in_specs=around(rows) + around(HALO) + around(HALO)
            + [
                main(rows),
                main(rows),
                pl.BlockSpec((1,) + down.shape[1:], lambda v, w: (v, 0, 0)),
                pl.BlockSpec((1,) + across.shape[1:], lambda v, w: (v, 0, 0, 0)),
                pl.BlockSpec(memory_space=pltpu.SMEM),
            ],
            out_specs=pl.BlockSpec((2, 1, rows, cols), lambda v, w: (0, v, 0, 0)),
            scratch_shapes=[pltpu.VMEM((3 * depth, cols + 2 * LANES), jnp.bfloat16)],
        ),
        out_shape=jax.ShapeDtypeStruct((2, visits, rows, cols), jnp.float32),
        name="match_block",
        cost_estimate=pl.CostEstimate(
            flops=visits * cols * 1000000,
            bytes_accessed=visits * rows * cols * 40,
            transcendentals=0,
        ),
    )(
        where, exposure, exposure, exposure, above, above, above, below, below, below,
        variance, usable, down, across, coef,
    )


def merge_kernel(*refs):
    *records, out = refs
    rows, cols = out.shape
    visits = records[0].shape[1]
    lanes = pl.ds
    for r in range(0, rows, 8):
        for c in range(0, cols, LANES):
            at = (slice(r, r + 8), slice(c, c + LANES))
            low = [jnp.full((8, LANES), big_value, jnp.float32)] * 3
            high = [jnp.full((8, LANES), -big_value, jnp.float32)] * 3
            for record in records:
                for v in range(visits):
                    value = record[(0, v) + at]
                    on = record[(1, v) + at] > 0.0
                    a = jnp.where(on, value, big_value)
                    b = jnp.where(on, value, -big_value)
                    a1 = jnp.maximum(low[0], a)
                    a2 = jnp.maximum(low[1], a1)
                    low = [jnp.minimum(low[0], a), jnp.minimum(low[1], a1), jnp.minimum(low[2], a2)]
                    b1 = jnp.minimum(high[0], b)
                    b2 = jnp.minimum(high[1], b1)
                    high = [jnp.maximum(high[0], b), jnp.maximum(high[1], b1), jnp.maximum(high[2], b2)]
            numer = jnp.zeros((8, LANES), jnp.float32)
            denom = jnp.zeros((8, LANES), jnp.float32)
            for record in records:
                for v in range(visits):
                    weight = record[(1, v) + at]
                    numer = numer + weight * jnp.clip(record[(0, v) + at], low[2], high[2])
                    denom = denom + weight
            out[at] = numer / denom


def merge(records):
    _, visits, rows, cols = records[0].shape
    wide = min(cols, 2 * LANES)
    spec = pl.BlockSpec((2, visits, rows, wide), lambda i: (0, 0, 0, i))
    return pl.pallas_call(
        merge_kernel,
        grid=(cols // wide,),
        in_specs=[spec] * len(records),
        out_specs=pl.BlockSpec((rows, wide), lambda i: (0, i)),
        out_shape=jax.ShapeDtypeStruct((rows, cols), jnp.float32),
        name="merge_visits",
    )(*records)


def assemble_kernel(where_ref, *refs):
    *blocks, out = refs
    for i, block in enumerate(blocks):
        @pl.when(pl.program_id(0) == i)
        def _():
            out[...] = block[...]


def assemble(where, blocks):
    rows, cols = blocks[0].shape
    count = len(blocks)
    return pl.pallas_call(
        assemble_kernel,
        grid_spec=pltpu.PrefetchScalarGridSpec(
            num_scalar_prefetch=1,
            grid=(count,),
            in_specs=[pl.BlockSpec((rows, cols), lambda i, w: (0, 0))] * count,
            out_specs=pl.BlockSpec((rows, cols), lambda i, w: (0, w[i])),
        ),
        out_shape=jax.ShapeDtypeStruct((rows, cols * count), jnp.float32),
        name="place_blocks",
    )(where, *blocks)


def per_device(exposure, variance, usable, basis_width, spatial_coef):
    visits_here, row_count, col_count = exposure.shape
    ranks = lax.axis_size("visit")
    tiles = lax.axis_size("tile")
    me = lax.axis_index("visit")
    tile_id = lax.axis_index("tile")
    cols = col_count // ranks
    ends = tiles - 1
    above = lax.ppermute(
        exposure[:, row_count - HALO :, :], "tile", [(i, i + 1) for i in range(ends)]
    )
    below = lax.ppermute(exposure[:, :HALO, :], "tile", [(i + 1, i) for i in range(ends)])
    down, across = prep(basis_width, row_count)

    def block(k):
        where = jnp.stack([lax.rem(me + k, ranks), tile_id]).astype(jnp.int32)
        return match(
            where, cols, row_count * tiles, exposure, above, below, variance, usable,
            down, across, spatial_coef,
        )

    def shift(array, k):
        return lax.ppermute(array, "visit", [(i, (i + k) % ranks) for i in range(ranks)])

    received = [shift(block(k), k) for k in range(1, ranks)]
    mine = merge([block(0)] + received)
    blocks = [mine] + [shift(mine, k) for k in range(1, ranks)]
    where = lax.rem(me - jnp.arange(ranks, dtype=jnp.int32) + ranks, ranks)
    return assemble(where, blocks)


def solution(mesh):
    in_specs = (
        P("visit", ("patch", "tile"), None),
        P("visit", ("patch", "tile"), None),
        P("visit", ("patch", "tile"), None),
        P(("patch", "visit"), None),
        P(("patch", "visit"), None, None),
    )
    out_specs = P(("patch", "tile"), None)
    return jax.shard_map(
        per_device, mesh=mesh, in_specs=in_specs, out_specs=out_specs, check_vma=False
    )
```
